256 devices in a mesh: section: 4 (over y), dp: 32 (over x, z), tensor: 2 (over core).
Axes of the slice: x: 4, y: 4, z: 8, core: 2. Of those that a mesh axis runs over, the one named last changes fastest.
Arguments:
- activations: bfloat16 [4, 32768, 5120], P('section', 'dp'), may hold values from -6 to 6
- cotangents: bfloat16 [4, 32768, 1024], P('section', 'dp', 'tensor'), may hold values from -25 to 25
- doc_ids: int32 [32, 1024], P('dp'), may hold values from 0 to 15, never falling along the last dimension, each value on 1 to 128 neighbouring positions
Outputs:
- clipped_grad: float32 [4, 5120, 1024], P('section', 'dp', 'tensor')
- clip_factor: float32 [32, 16], P('dp')
The draws below stay inside these ranges and needn't reach their ends.
Inputs may be any that keep to these rules, and one draw needn't show every extreme that they name: `doc_ids`: in each row the numbers never fall, every number 0 to 15 occurs, and each document has 1 to 128 tokens, one exactly 128.
All inputs are finite; a program needn't handle non-finite values.
Results may differ from the reference program's by a relative error of at most 0.0003.
Values may be sent and summed in bfloat16 or wider, within the bound.
A program may use at most 128 MiB of HBM per device.

```python
import math
import jax
import jax.numpy as jnp
import numpy as np
from jax import lax

D = 5120
KV = 1024
LENGTH = 1024
DOCS = 16
MOST = 128
CLIP_TOK = 192
SECTIONS = 4
ROWS = 32
TOKENS = 32768


def shared_mixing(key):
    return jax.random.normal(jax.random.fold_in(key, 31), (SECTIONS, TOKENS, 8), jnp.float32)


def mixed_values(key, mixing, width, basis_tag, noise_tag):
    basis = jax.random.normal(jax.random.fold_in(key, basis_tag), (SECTIONS, 8, width), jnp.float32)
    common = jnp.einsum('str,srd->std', mixing, basis, precision=lax.Precision.HIGHEST)
    noise = jax.random.normal(jax.random.fold_in(key, noise_tag), (SECTIONS, TOKENS, width), jnp.float32)
    return 0.70710678 * noise + 0.25 * common


def draw_activations(key, part):
    mixing = shared_mixing(key)
    values = mixed_values(key, mixing, D, 32, 33)
    return jnp.clip(values, -6.0, 6.0).astype(jnp.bfloat16)


def draw_cotangents(key, part):
    mixing = shared_mixing(key)
    values = mixed_values(key, mixing, KV, 34, 35)
    section_scale = 1.0 + 2.0 * jnp.arange(SECTIONS, dtype=jnp.float32) / max(SECTIONS - 1, 1)
    position = jnp.arange(KV, dtype=jnp.float32) / max(KV - 1, 1)
    column_scale = jnp.sqrt((1.0 + 8.0 * position) / 5.0)
    values = jnp.clip(values, -6.0, 6.0)
    return (values * section_scale[:, None, None] * column_scale[None, None, :]).astype(jnp.bfloat16)


def profile(amount, total, reach, skew):
    portions = [(1 << 20) // math.isqrt(rank ** skew) + 1 for rank in range(2, amount + 1)]
    surplus, counts = total - reach - (amount - 1), [1] * (amount - 1)
    while surplus > 0:
        movable = [i for i in range(amount - 1) if counts[i] < reach]
        mass, left = sum([portions[i] for i in movable]), surplus
        for i in movable:
            addition = min(reach - counts[i], max(1, left * portions[i] // mass), surplus)
            counts[i] = counts[i] + addition
            surplus = surplus - addition
    return np.array([reach] + counts)


def uneven_parts(rng, amount, total, most, skew):
    if amount == 2:
        one = jax.random.randint(rng, (), max(1, total - most), min(most, total - 1) + 1)
        return jnp.stack([one, total - one])
    tallies = jnp.asarray(profile(amount, total, most, skew), jnp.int32)
    pairs = (amount - 1) // 2
    source_of, receiver = tallies[1:1 + 2 * pairs:2], tallies[2:2 + 2 * pairs:2]
    margin = jnp.minimum(source_of - 1, most - receiver)
    shifted = jax.random.randint(jax.random.fold_in(rng, 1), (pairs,), 0, 1 << 20) % (margin + 1)
    tallies = tallies.at[1:1 + 2 * pairs:2].set(source_of - shifted).at[2:2 + 2 * pairs:2].set(receiver + shifted)
    return tallies[jax.random.permutation(jax.random.fold_in(rng, 2), amount)]


def setup_inputs(seed: int = 0) -> dict:
    arg_keys = jax.random.split(jax.random.key(seed), 4)
    activations = draw_activations(jax.random.fold_in(arg_keys[3], 71), 0)
    cotangents = draw_cotangents(jax.random.fold_in(arg_keys[3], 71), 0)
    doc_ids = jax.vmap(lambda own: jnp.searchsorted(jnp.cumsum(uneven_parts(own, DOCS, LENGTH, MOST, 1)), jnp.arange(LENGTH), side="right"))(jax.random.split(arg_keys[2], ROWS)).reshape((ROWS, LENGTH)).astype(jnp.int32)
    return dict(activations=activations, cotangents=cotangents, doc_ids=doc_ids)


def tile_rows(activ, cotan, doc_tok):
    length = activ.shape[0]
    count = length // 128
    act_tiles = activ.astype(jnp.float32).reshape(count, 128, activ.shape[1])
    cot_tiles = cotan.astype(jnp.float32).reshape(count, 128, cotan.shape[1])
    id_tiles = doc_tok.reshape(count, 128)
    act_diag = jnp.einsum('ntd,nsd->nts', act_tiles, act_tiles)
    cot_diag = jnp.einsum('ntd,nsd->nts', cot_tiles, cot_tiles)
    same_diag = id_tiles[:, :, None] == id_tiles[:, None, :]
    row_sums = lax.optimization_barrier(jnp.sum(jnp.where(same_diag, act_diag * cot_diag, jnp.float32(0.0)), axis=2))
    if count > 1:
        act_next = jnp.einsum('ntd,nsd->nts', act_tiles[:-1], act_tiles[1:])
        cot_next = jnp.einsum('ntd,nsd->nts', cot_tiles[:-1], cot_tiles[1:])
        same_next = id_tiles[:-1, :, None] == id_tiles[1:, None, :]
        product = jnp.where(same_next, act_next * cot_next, jnp.float32(0.0))
        zero_row = jnp.zeros((1, 128), jnp.float32)
        row_sums = row_sums + jnp.concatenate([lax.optimization_barrier(jnp.sum(product, axis=2)), zero_row], axis=0)
        row_sums = row_sums + jnp.concatenate([zero_row, lax.optimization_barrier(jnp.sum(product, axis=1))], axis=0)
    return row_sums.reshape(length)

def reference(activations, cotangents, doc_ids):
    doc_range = jnp.arange(DOCS, dtype=jnp.int32)
    one_hot = (doc_ids[:, :, None] == doc_range[None, None, :]).astype(jnp.float32)
    norm_sq = jnp.zeros((ROWS, DOCS), jnp.float32)
    for section in range(SECTIONS):
        act_rows = activations[section].reshape(ROWS, LENGTH, D)
        cot_rows = cotangents[section].reshape(ROWS, LENGTH, KV)
        row_sums = lax.map(lambda triple: tile_rows(triple[0], triple[1], triple[2]), (act_rows, cot_rows, doc_ids))
        norm_sq = norm_sq + lax.optimization_barrier(jnp.sum(one_hot * row_sums[:, :, None], axis=1))
    bound = math.sqrt(4.0 * CLIP_TOK * SECTIONS * D * KV)
    clip_factor = jnp.minimum(jnp.float32(1.0), bound * lax.rsqrt(norm_sq + 1e-06))
    scale = 1.0 / math.sqrt(ROWS * LENGTH)
    token_factor = jnp.take_along_axis(clip_factor, doc_ids, axis=1).reshape(TOKENS) * scale
    grads = []
    for section in range(SECTIONS):
        scaled = (cotangents[section].astype(jnp.float32) * token_factor[:, None]).astype(jnp.bfloat16)
        grads.append(jnp.dot(activations[section].T, scaled, preferred_element_type=jnp.float32))
    return (jnp.stack(grads), clip_factor)
```

```python
import functools
import math

import jax
import jax.numpy as jnp
from jax import lax
from jax.experimental import pallas as pl
from jax.experimental.pallas import tpu as pltpu
from jax.sharding import PartitionSpec as P

D = 5120
KV = 1024
DOCS = 16
CLIP_TOK = 192

F32 = jnp.float32
BF16 = jnp.bfloat16
I16 = jnp.int16
MESH = pl.DeviceIdType.MESH
TOP = 32767.0
TINY = 1e-30

NX, NZ = 4, 8
BLOCK = D // (NX * NZ)
ROWS1, ROWS2 = 96, 64
H1, H2 = ROWS1 // 2, ROWS2 // 2
STEPS = NZ
LAG_B, LAG_C = 2, 4


def nt(a, b):
    return lax.dot_general(a, b, (((1,), (1,)), ((), ())), preferred_element_type=F32)


def tn(a, b, precision=None):
    return lax.dot_general(a, b, (((0,), (0,)), ((), ())), preferred_element_type=F32, precision=precision)


def zeta(z, p):
    odd = p % 2
    return (z + 4 + (1 - odd) * (p // 2) - odd * ((p + 1) // 2)) % NZ


def kernel(
    a_hbm, g_hbm, ids_ref, out_ref, clip_ref,
    a, at, g, gp, part, scaled, norms,
    xs1, xr1, xss1, xrs1, zs1, zr1, zss1, zrs1,
    xs2, xr2, xss2, xrs2, zs2, zr2, zss2, zrs2,
    a_sem, g_sem, gp_send, gp_recv, n_send, n_recv,
    x1_send, x1_recv, z1_send, z1_recv, x2_send, x2_recv, z2_send, z2_recv,
):
    length = a.shape[0]
    sections = lax.axis_size("section")
    y, dp, core = lax.axis_index("section"), lax.axis_index("dp"), lax.axis_index("tensor")
    x, z = dp // NZ, dp % NZ

    def at_x(step):
        return (y, ((x + step) % NX) * NZ + z, core)

    def at_z(step):
        return (y, x * NZ + (z + step) % NZ, core)

    group = [((y + i) % sections, dp, (core + j) % 2) for i in range(4) for j in range(2) if i or j]
    barrier = pltpu.get_barrier_semaphore()
    for peer in group + [at_x(1), at_x(NX - 1), at_z(1), at_z(NZ - 1)]:
        pl.semaphore_signal(barrier, inc=1, device_id=peer, device_id_type=MESH)

    chunks = length // 128

    def a_copy(i):
        row = pl.multiple_of(((i + 3 * core) % chunks) * 128, 128)
        return pltpu.make_async_copy(a_hbm.at[pl.ds(row, 128)], a.at[pl.ds(row, 128)], a_sem.at[i])

    g_copy = pltpu.make_async_copy(g_hbm, g, g_sem)
    g_copy.start()
    for i in range(chunks):
        a_copy(i).start()
    pl.semaphore_wait(barrier, len(group) + 4)

    other_row = pl.multiple_of(384 * (1 - core), 128)
    gp_copy = pltpu.make_async_remote_copy(
        g_hbm.at[pl.ds(other_row, 640)], gp.at[pl.ds(other_row, 640)], gp_send, gp_recv,
        device_id=(y, dp, 1 - core), device_id_type=MESH,
    )
    gp_copy.start()

    one_hot = (lax.broadcasted_iota(jnp.int32, (DOCS, length), 0) == ids_ref[...]).astype(F32)

    hot_ref = norms.at[2 * sections]
    for k in range(length // 128):
        norms[2 * sections + k] = one_hot[:, k * 128 : (k + 1) * 128]
    del hot_ref

    def hot(first, count):
        return jnp.concatenate([norms[2 * sections + first + k] for k in range(count)], axis=1)

    g_copy.wait()
    for i in range(3):
        a_copy(i).wait()
    total = jnp.zeros((DOCS, 256), F32)
    for j in range(2):
        if j == 1:
            for i in range(3, 5):
                a_copy(i).wait()
        u0 = pl.multiple_of(512 * core + 256 * j, 128)
        t0 = pl.multiple_of(jnp.maximum(u0 - 128, 0), 128)
        act = nt(a[pl.ds(t0, 384), :], a[pl.ds(u0, 256), :])
        if j == 0:
            gp_copy.wait_recv()
        cot = nt(g[pl.ds(t0, 384), :], g[pl.ds(u0, 256), :]) + nt(gp[pl.ds(t0, 384), :], gp[pl.ds(u0, 256), :])
        hot_u = hot(u0 // 128, 2)
        same = tn(hot(t0 // 128, 3), hot_u)
        t = lax.broadcasted_iota(jnp.int32, (384, 256), 0) + t0
        weight = jnp.where(t < u0, 2.0, jnp.where(t < u0 + 256, 1.0, 0.0))
        product = jnp.where(same > 0.5, act * cot * weight, 0.0)
        total = total + hot_u * jnp.sum(product, axis=0, keepdims=True)
    mine = y * 2 + core
    norms[mine] = total[:, :128] + total[:, 128:]
    n_copies = [
        pltpu.make_async_remote_copy(
            norms.at[mine], norms.at[mine], n_send.at[i], n_recv.at[i], device_id=peer, device_id_type=MESH
        )
        for i, peer in enumerate(group)
    ]
    for copy in n_copies:
        copy.start()

    for i in range(5, chunks):
        a_copy(i).wait()

    def transpose(i, _):
        lane = pl.multiple_of(i * 128, 128)
        at[pl.ds(lane, 128), :] = a[:, pl.ds(lane, 128)].T
        return 0

    lax.fori_loop(0, D // 128, transpose, 0)

    for copy in n_copies:
        copy.wait_recv()
    norm_sq = norms[0]
    for i in range(1, 2 * sections):
        norm_sq = norm_sq + norms[i]
    norm_sq = jnp.broadcast_to(jnp.sum(norm_sq, axis=1, keepdims=True), (DOCS, 128))
    bound = math.sqrt(4.0 * CLIP_TOK * sections * D * KV)
    clip = jnp.minimum(1.0, bound * lax.rsqrt(norm_sq + 1e-06))
    clip_ref[...] = clip.T[:1, :]
    factor = clip * (1.0 / math.sqrt(NX * NZ * length))
    for k in range(length // 128):
        fac = tn(norms[2 * sections + k], factor, lax.Precision.HIGHEST)
        for lane in range(0, KV // 2, 128):
            own = g[k * 128 : (k + 1) * 128, lane : lane + 128].astype(F32)
            scaled[k * 128 : (k + 1) * 128, lane : lane + 128] = (own * fac).astype(BF16)

    def base(x_of, z_of):
        return (x_of * NZ + z_of) * BLOCK

    def multiply(p):
        def one(i, _):
            row = pl.multiple_of(base(i, zeta(z, p)), 32)
            part[pl.ds(row, BLOCK), :] = jnp.dot(at[pl.ds(row, BLOCK), :], scaled[...], preferred_element_type=F32)
            return 0

        lax.fori_loop(0, NX, one, 0)

    def pieces(rows):
        return range(0, rows, 16)

    def decode(code, scale):
        return code.astype(jnp.int32).astype(F32) * scale

    def fold(m, value):
        value = jnp.abs(value)
        for r in range(0, value.shape[0], 8):
            for c in range(0, value.shape[1], 128):
                m = jnp.maximum(m, value[r : r + 8, c : c + 128])
        return m

    def spread(scale, like):
        return jnp.concatenate([scale] * (like // 128), axis=1)

    def encode(rows, count, code, scale_ref, add=None):
        m = jnp.zeros((8, 128), F32)
        for b, row in enumerate(rows):
            for r in pieces(count):
                value = part[pl.ds(pl.multiple_of(row + r, 16), 16), :]
                if add is not None:
                    value = value + add(b, r)
                    part[pl.ds(pl.multiple_of(row + r, 16), 16), :] = value
                m = fold(m, value)
        m = jnp.maximum(jnp.max(m, axis=0, keepdims=True), TINY)
        scale_ref[...] = jnp.broadcast_to(m * (1.0 / TOP), (8, 128))
        inverse = spread(TOP / m, KV // 2)
        for b, row in enumerate(rows):
            for r in pieces(count):
                value = part[pl.ds(pl.multiple_of(row + r, 16), 16), :]
                code[b * count + r : b * count + r + 16, :] = jnp.round(value * inverse).astype(jnp.int32).astype(I16)

    def adder(count, code, scale_ref):
        scale = spread(scale_ref[0:1, :], KV // 2)
        return lambda b, r: decode(code[b * count + r : b * count + r + 16, :], scale)

    def send(code, scale, to_code, to_scale, send_sem, recv_sem, peer):
        return (
            pltpu.make_async_remote_copy(code, to_code, send_sem.at[0], recv_sem.at[0], device_id=peer, device_id_type=MESH),
            pltpu.make_async_remote_copy(
                scale, to_scale, send_sem.at[1], recv_sem.at[1], device_id=peer, device_id_type=MESH
            ),
        )

    def start(copies):
        for copy in copies:
            copy.start()

    def landed(copies):
        for copy in copies:
            copy.wait_recv()

    class Ring:
        def __init__(self, half, first, bufs, sems):
            self.half, self.first = half, first
            self.code, self.got, self.scale, self.got_scale = bufs
            self.send_sem, self.recv_sem = sems

        def copies(self, p, way, unit):
            return send(
                self.code.at[p, way, unit], self.scale.at[p, way, unit, 0:1],
                self.got.at[p, way, unit], self.got_scale.at[p, way, unit, 0:1],
                self.send_sem.at[p, way, unit], self.recv_sem.at[p, way, unit], at_x(1 if way == 0 else NX - 1),
            )

        def row(self, step, z_of, half):
            return base((x + step) % NX, z_of) + self.first + half * self.half

        def own(self, p, z_of):
            for unit in range(2):
                for way in range(2):
                    step = 2 if unit == 0 else (1 if way == 0 else NX - 1)
                    half = way if unit == 0 else 1 - way
                    encode(
                        [self.row(step, z_of, half)], self.half, self.code.at[p, way, unit], self.scale.at[p, way, unit]
                    )
                    start(self.copies(p, way, unit))

        def pass_on(self, p, z_of):
            for way in range(2):
                landed(self.copies(p, way, 0))
                encode(
                    [self.row(1 if way == 0 else NX - 1, z_of, way)], self.half,
                    self.code.at[p, way, 2], self.scale.at[p, way, 2],
                    adder(self.half, self.got.at[p, way, 0], self.got_scale.at[p, way, 0]),
                )
                start(self.copies(p, way, 2))

        def finish(self, p, z_of, put):
            for unit in (1, 2):
                for way in range(2):
                    landed(self.copies(p, way, unit))
            for half in range(2):
                one = adder(self.half, self.got.at[p, half, 2], self.got_scale.at[p, half, 2])
                two = adder(self.half, self.got.at[p, 1 - half, 1], self.got_scale.at[p, 1 - half, 1])
                row = self.row(0, z_of, half)
                for r in pieces(self.half):
                    value = part[pl.ds(pl.multiple_of(row + r, 16), 16), :] + one(0, r) + two(0, r)
                    put(row, half, r, value)

        def drain(self, steps):
            def one(p, _):
                for way in range(2):
                    for unit in range(3):
                        for copy in self.copies(p, way, unit):
                            copy.wait_send()
                return 0

            lax.fori_loop(0, steps, one, 0)

    class Chain:
        def __init__(self, half, first, blocks, bufs, sems):
            self.half, self.first, self.blocks = half, first, blocks
            self.code, self.got, self.scale, self.got_scale = bufs
            self.send_sem, self.recv_sem = sems

        def rows(self, z_of, half):
            return [base(b, z_of) + self.first + half * self.half for b in self.blocks]

        def copies(self, p, half, slot, step):
            return send(
                self.code.at[p, half], self.scale.at[p, half, 0:1], self.got.at[slot, half], self.got_scale.at[slot, half, 0:1],
                self.send_sem.at[p, half], self.recv_sem.at[slot, half], at_z(step),
            )

        def clear(self):
            for slot, half in ((0, 1), (1, 0)):
                self.got_scale[slot, half] = jnp.zeros((8, 128), F32)

        def begin(self):
            for half in range(2):
                encode(self.rows(zeta(z, 0), half), self.half, self.code.at[0, half], self.scale.at[0, half])
                start(self.copies(0, half, half, 1 if half == 0 else NZ - 1))

        def step(self, p):
            odd = p % 2
            for half in (odd, 1 - odd):

                def arrived(half=half):
                    landed(self.copies(p, half, p - 1, 1))

                if half is odd:
                    pl.when(p >= 3)(arrived)
                else:
                    arrived()
                encode(
                    self.rows(zeta(z, p), half), self.half, self.code.at[p, half], self.scale.at[p, half],
                    adder(self.half, self.got.at[p - 1, half], self.got_scale.at[p - 1, half]),
                )
                start(self.copies(p, half, p + 1, 1 + (1 - odd) * (NZ - 2)))

        def finish(self, put):
            for slot in (NZ - 2, NZ - 1):
                for half in range(2):
                    landed(self.copies(0, half, slot, 1))
            for half in range(2):
                one = adder(self.half, self.got.at[NZ - 2, half], self.got_scale.at[NZ - 2, half])
                two = adder(self.half, self.got.at[NZ - 1, half], self.got_scale.at[NZ - 1, half])
                for b, row in enumerate(self.rows(z, half)):
                    for r in pieces(self.half):
                        value = part[pl.ds(pl.multiple_of(row + r, 16), 16), :] + one(b, r) + two(b, r)
                        put(row, half, r, value)

        def drain(self):
            def one(p, _):
                for half in range(2):
                    for copy in self.copies(p, half, 0, 1):
                        copy.wait_send()
                return 0

            lax.fori_loop(0, NZ - 1, one, 0)

    ring1 = Ring(H1, 0, (xs1, xr1, xss1, xrs1), (x1_send, x1_recv))
    chain1 = Chain(H1, 0, [x], (zs1, zr1, zss1, zrs1), (z1_send, z1_recv))
    ring2 = Ring(H2, ROWS1, (xs2, xr2, xss2, xrs2), (x2_send, x2_recv))
    chain2 = Chain(H2, ROWS1, list(range(NX)), (zs2, zr2, zss2, zrs2), (z2_send, z2_recv))

    def keep(row, half, r, value):
        part[pl.ds(pl.multiple_of(row + r, 16), 16), :] = value

    def put1(row, half, r, value):
        out_ref[half * H1 + r : half * H1 + r + 16, :] = value

    def put2(row, half, r, value):
        out_ref[ROWS1 + half * H2 + r : ROWS1 + half * H2 + r + 16, :] = value

    chain1.clear()
    chain2.clear()

    def turn(s, _):
        @pl.when(s < STEPS)
        def _():
            multiply(s)
            ring1.own(s, zeta(z, s))

        pl.when(s == 0)(chain2.begin)

        @pl.when((s >= 1) & (s <= STEPS - 2))
        def _():
            chain2.step(s)

        @pl.when(s == STEPS - 1)
        def _():
            chain2.finish(keep)
            ring2.own(0, z)

        @pl.when((s >= LAG_B) & (s < STEPS + LAG_B))
        def _():
            ring1.pass_on(s - LAG_B, zeta(z, s - LAG_B))

        pl.when(s == STEPS)(lambda: ring2.pass_on(0, z))
        pl.when(s == STEPS + 1)(lambda: ring2.finish(0, z, put2))

        @pl.when(s >= LAG_C)
        def _():
            ring1.finish(s - LAG_C, zeta(z, s - LAG_C), keep)

        pl.when(s == LAG_C)(chain1.begin)

        @pl.when((s > LAG_C) & (s < STEPS + LAG_C - 1))
        def _():
            chain1.step(s - LAG_C)

        return 0

    lax.fori_loop(0, STEPS + LAG_C, turn, 0)
    chain1.finish(put1)

    gp_copy.wait_send()
    for copy in n_copies:
        copy.wait_send()
    ring1.drain(STEPS)
    chain1.drain()
    ring2.drain(1)
    chain2.drain()


def per_device(activations, cotangents, doc_ids):
    length, half_kv = activations.shape[1], cotangents.shape[2]
    sections = lax.axis_size("section")
    dma = pltpu.SemaphoreType.DMA
    units1, units2 = (STEPS, 2, 3), (1, 2, 3)
    hops = (STEPS, 2)

    def buffers(shape, rows):
        return [pltpu.VMEM(shape + (rows, half_kv), I16)] * 2 + [pltpu.VMEM(shape + (8, 128), F32)] * 2

    grad, clip = pl.pallas_call(
        kernel,
        out_shape=(
            jax.ShapeDtypeStruct((BLOCK, half_kv), F32),
            jax.ShapeDtypeStruct((1, DOCS), F32),
        ),
        in_specs=[
            pl.BlockSpec(memory_space=pl.ANY),
            pl.BlockSpec(memory_space=pl.ANY),
            pl.BlockSpec(memory_space=pltpu.VMEM),
        ],
        out_specs=[pl.BlockSpec(memory_space=pltpu.VMEM)] * 2,
        scratch_shapes=[
            pltpu.VMEM((length, D), BF16),
            pltpu.VMEM((D, length), BF16),
            pltpu.VMEM((length, half_kv), BF16),
            pltpu.VMEM((length, half_kv), BF16),
            pltpu.VMEM((D, half_kv), F32),
            pltpu.VMEM((length, half_kv), BF16),
            pltpu.VMEM((2 * sections + length // 128, DOCS, 128), F32),
            *buffers(units1, H1),
            *buffers(hops, H1),
            *buffers(units2, H2),
            *buffers(hops, NX * H2),
            dma((length // 128,)),
            dma(()),
            dma(()),
            dma(()),
            dma((7,)),
            dma((7,)),
            dma(units1 + (2,)),
            dma(units1 + (2,)),
            dma(hops + (2,)),
            dma(hops + (2,)),
            dma(units2 + (2,)),
            dma(units2 + (2,)),
            dma(hops + (2,)),
            dma(hops + (2,)),
        ],
        compiler_params=pltpu.CompilerParams(
            collective_id=0, has_side_effects=True, vmem_limit_bytes=63 << 20
        ),
        name="clip_and_reduce",
    )(activations[0], cotangents[0], doc_ids)
    return grad[None], clip


def solution(mesh):
    return jax.shard_map(
        per_device,
        mesh=mesh,
        in_specs=(P("section", "dp", None), P("section", "dp", "tensor"), P("dp", None)),
        out_specs=(P("section", "dp", "tensor"), P("dp", None)),
        check_vma=False,
    )
```

```python
import functools
import math

import jax
import jax.numpy as jnp
from jax import lax
from jax.experimental import pallas as pl
from jax.experimental.pallas import tpu as pltpu
from jax.sharding import PartitionSpec as P

D = 5120
KV = 1024
DOCS = 16
CLIP_TOK = 192

F32 = jnp.float32
BF16 = jnp.bfloat16
I16 = jnp.int16
MESH = pl.DeviceIdType.MESH
TOP = 32767.0
TINY = 1e-30

NX, NZ = 4, 8
BLOCK = D // (NX * NZ)
ROWS1, ROWS2 = 96, 64
H1, H2 = ROWS1 // 2, ROWS2 // 2
STEPS = NZ
K_CHUNK = 1280
TRANSPOSE_EARLY = True
ORDER = (
    "M0", "A0", "H00", "M1", "H10", "A1", "M2", "H20", "A2", "M3", "B0", "A3", "M4", "H11", "H21", "A4", "M5", "B1", "M6",
    "H30", "B2", "A5", "H40", "M7", "C0", "Z0", "A7", "A6", "H31", "H41", "B3", "H50", "H60", "B4", "C1", "Z1", "C2", "Z2",
    "H51", "H61", "B5", "B7", "B6", "C3", "Z3", "C4", "Z4", "E", "F", "C5", "C7", "Z5", "C6", "Z6", "G", "I",
)


def nt(a, b):
    return lax.dot_general(a, b, (((1,), (1,)), ((), ())), preferred_element_type=F32)


def tn(a, b, precision=None):
    return lax.dot_general(a, b, (((0,), (0,)), ((), ())), preferred_element_type=F32, precision=precision)


def zeta(z, p):
    odd = p % 2
    return (z + 4 + (1 - odd) * (p // 2) - odd * ((p + 1) // 2)) % NZ


def kernel(
    a_hbm, g_hbm, ids_ref, out_ref, clip_ref,
    a, at, g, gp, part, scaled, norms, acts, cots,
    xs1, xr1, xss1, xrs1, zs1, zr1, zss1, zrs1,
    xs2, xr2, xss2, xrs2, zs2, zr2, zss2, zrs2,
    a_sem, g_sem, gp_sem, n_send, n_recv, sent, x1_recv, z1_recv, x2_recv, z2_recv,
):
    length = a.shape[0]
    sections = lax.axis_size("section")
    y, dp, core = lax.axis_index("section"), lax.axis_index("dp"), lax.axis_index("tensor")
    x, z = dp // NZ, dp % NZ

    def at_x(step):
        return (y, ((x + step) % NX) * NZ + z, core)

    def at_z(step):
        return (y, x * NZ + (z + step) % NZ, core)

    group = [((y + i) % sections, dp, (core + j) % 2) for i in range(4) for j in range(2) if i or j]
    barrier = pltpu.get_barrier_semaphore()
    for peer in group + [at_x(1), at_x(NX - 1), at_z(1), at_z(NZ - 1)]:
        pl.semaphore_signal(barrier, inc=1, device_id=peer, device_id_type=MESH)

    chunks = D // K_CHUNK
    first = pl.multiple_of(384 * core, 128)
    rest = pl.multiple_of(640 * (1 - core), 128)

    def a_copy(k):
        if k < chunks:
            where = (pl.ds(first, 640), pl.ds(k * K_CHUNK, K_CHUNK))
        else:
            where = (pl.ds(pl.multiple_of(rest + 128 * (k - chunks), 128), 128), pl.ds(0, D))
        return pltpu.make_async_copy(a_hbm.at[where], a.at[where], a_sem.at[k])

    g_copy = pltpu.make_async_copy(g_hbm, g, g_sem)
    g_copy.start()
    for k in range(2):
        a_copy(k).start()
    pl.semaphore_wait(barrier, len(group) + 4)

    other_row = pl.multiple_of(384 * (1 - core), 128)
    gp_copy = pltpu.make_async_remote_copy(
        g_hbm.at[pl.ds(other_row, 640)], gp.at[pl.ds(other_row, 640)], gp_sem.at[0], gp_sem.at[1],
        device_id=(y, dp, 1 - core), device_id_type=MESH,
    )
    gp_copy.start()

    one_hot = (lax.broadcasted_iota(jnp.int32, (DOCS, length), 0) == ids_ref[...]).astype(F32)
    for k in range(length // 128):
        norms[2 * sections + k] = one_hot[:, k * 128 : (k + 1) * 128]

    def hot(start, count):
        return jnp.concatenate([norms[2 * sections + start + k] for k in range(count)], axis=1)

    def tokens(j):
        u0 = pl.multiple_of(512 * core + 256 * j, 128)
        return pl.multiple_of(jnp.maximum(u0 - 128, 0), 128), u0

    g_copy.wait()
    for j in range(2):
        t0, u0 = tokens(j)
        cots[j] = nt(g[pl.ds(t0, 384), :], g[pl.ds(u0, 256), :])

    for k in range(chunks):
        a_copy(k).wait()
        if k + 2 < chunks:
            a_copy(k + 2).start()
        elif k + 2 == chunks:
            for i in range(3):
                a_copy(chunks + i).start()
        column = k * K_CHUNK
        for j in range(2):
            t0, u0 = tokens(j)
            product = nt(a[pl.ds(t0, 384), pl.ds(column, K_CHUNK)], a[pl.ds(u0, 256), pl.ds(column, K_CHUNK)])
            acts[j] = product if k == 0 else acts[j] + product
        for lane in range(column, column + K_CHUNK, 128) if TRANSPOSE_EARLY else ():
            at[lane : lane + 128, pl.ds(first, 640)] = a[pl.ds(first, 640), lane : lane + 128].T

    gp_copy.wait_recv()
    total = jnp.zeros((DOCS, 256), F32)
    for j in range(2):
        t0, u0 = tokens(j)
        cot = cots[j] + nt(gp[pl.ds(t0, 384), :], gp[pl.ds(u0, 256), :])
        hot_u = hot(u0 // 128, 2)
        same = tn(hot(t0 // 128, 3), hot_u)
        t = lax.broadcasted_iota(jnp.int32, (384, 256), 0) + t0
        weight = jnp.where(t < u0, 2.0, jnp.where(t < u0 + 256, 1.0, 0.0))
        product = jnp.where(same > 0.5, acts[j] * cot * weight, 0.0)
        total = total + hot_u * jnp.sum(product, axis=0, keepdims=True)
    mine = y * 2 + core
    norms[mine] = total[:, :128] + total[:, 128:]
    n_copies = [
        pltpu.make_async_remote_copy(
            norms.at[mine], norms.at[mine], n_send, n_recv.at[i], device_id=peer, device_id_type=MESH
        )
        for i, peer in enumerate(group)
    ]
    for copy in n_copies:
        copy.start()

    for i in range(3):
        a_copy(chunks + i).wait()

    def transpose(i, _):
        lane = pl.multiple_of(i * 128, 128)
        if not TRANSPOSE_EARLY:
            at[pl.ds(lane, 128), pl.ds(first, 640)] = a[pl.ds(first, 640), pl.ds(lane, 128)].T
        at[pl.ds(lane, 128), pl.ds(rest, 384)] = a[pl.ds(rest, 384), pl.ds(lane, 128)].T
        return 0

    lax.fori_loop(0, D // 128, transpose, 0)

    for copy in n_copies:
        copy.wait_recv()
    norm_sq = norms[0]
    for i in range(1, 2 * sections):
        norm_sq = norm_sq + norms[i]
    norm_sq = jnp.broadcast_to(jnp.sum(norm_sq, axis=1, keepdims=True), (DOCS, 128))
    bound = math.sqrt(4.0 * CLIP_TOK * sections * D * KV)
    clip = jnp.minimum(1.0, bound * lax.rsqrt(norm_sq + 1e-06))
    clip_ref[...] = clip.T[:1, :]
    factor = clip * (1.0 / math.sqrt(NX * NZ * length))
    for k in range(length // 128):
        fac = tn(norms[2 * sections + k], factor, lax.Precision.HIGHEST)
        for lane in range(0, KV // 2, 128):
            own = g[k * 128 : (k + 1) * 128, lane : lane + 128].astype(F32)
            scaled[k * 128 : (k + 1) * 128, lane : lane + 128] = (own * fac).astype(BF16)

    def base(x_of, z_of):
        return (x_of * NZ + z_of) * BLOCK

    def multiply(p):
        def one(i, _):
            row = pl.multiple_of(base(i, zeta(z, p)), 32)
            part[pl.ds(row, BLOCK), :] = jnp.dot(at[pl.ds(row, BLOCK), :], scaled[...], preferred_element_type=F32)
            return 0

        lax.fori_loop(0, NX, one, 0)

    def at_row(row, r):
        return pl.ds(pl.multiple_of(row + r, 16), 16)

    def pieces(rows):
        return range(0, rows, 16)

    def loop(count, body, carry):
        return body(0, carry) if count == 1 else lax.fori_loop(0, count, body, carry)

    def fold(m, value):
        value = jnp.abs(value)
        for r in range(0, value.shape[0], 8):
            for c in range(0, value.shape[1], 128):
                m = jnp.maximum(m, value[r : r + 8, c : c + 128])
        return m

    def spread(scale):
        return jnp.concatenate([scale] * (KV // 2 // 128), axis=1)

    def encode(row_of, blocks, count, code, scale_ref, add=None):
        def largest(b, m):
            for r in pieces(count):
                value = part[at_row(row_of(b), r), :]
                if add is not None:
                    value = value + add(b, r)
                    part[at_row(row_of(b), r), :] = value
                m = fold(m, value)
            return m

        m = loop(blocks, largest, jnp.zeros((8, 128), F32))
        m = jnp.maximum(jnp.max(m, axis=0, keepdims=True), TINY)
        scale_ref[...] = jnp.broadcast_to(m * (1.0 / TOP), (8, 128))
        inverse = spread(TOP / m)

        def put(b, _):
            for r in pieces(count):
                value = part[at_row(row_of(b), r), :]
                code[at_row(b * count, r), :] = jnp.round(value * inverse).astype(jnp.int32).astype(I16)
            return 0

        loop(blocks, put, 0)

    def adder(count, code, scale_ref):
        scale = spread(scale_ref[0:1, :])
        return lambda b, r: code[at_row(b * count, r), :].astype(jnp.int32).astype(F32) * scale

    def message(bufs, there, here, slot, kind, recv_sem, peer):
        code, got, scale, got_scale = bufs
        one = (slice(0, 1),)
        return [
            pltpu.make_async_remote_copy(
                code.at[here], got.at[there], sent.at[kind, 0], recv_sem.at[slot + (0,)], device_id=peer, device_id_type=MESH
            ),
            pltpu.make_async_remote_copy(
                scale.at[here + one], got_scale.at[there + one], sent.at[kind, 1], recv_sem.at[slot + (1,)],
                device_id=peer, device_id_type=MESH,
            ),
        ]

    def start(copies):
        for copy in copies:
            copy.start()

    def landed(copies):
        for copy in copies:
            copy.wait_recv()

    def drain(bufs, kind):
        everything = (slice(None),) * (len(bufs[2].shape) - 2)
        for i, ref in enumerate((bufs[0], bufs[2].at[everything + (slice(0, 1),)])):
            pltpu.make_async_remote_copy(
                ref, ref, sent.at[kind, i], sent.at[kind, i], device_id=at_x(1), device_id_type=MESH
            ).wait_send()

    class Ring:
        def __init__(self, half, first, bufs, recv_sem, kind):
            self.half, self.first, self.bufs, self.recv_sem, self.kind = half, first, bufs, recv_sem, kind

        def copies(self, p, way, late):
            units = (p, way, pl.ds(2, 1) if late else pl.ds(0, 2))
            return message(self.bufs, units, units, (p, way, late), self.kind, self.recv_sem, at_x(1 + 2 * way))

        def row(self, step, z_of, half):
            return base((x + step) % NX, z_of) + self.first + half * self.half

        def own(self, p, z_of):
            def one(way, _):
                for unit in range(2):
                    row = self.row(1 + 2 * way, z_of, 1 - way) if unit else self.row(2, z_of, way)
                    encode(lambda b: row, 1, self.half, self.bufs[0].at[p, way, unit], self.bufs[2].at[p, way, unit])
                start(self.copies(p, way, 0))
                return 0

            lax.fori_loop(0, 2, one, 0)

        def pass_on(self, p, z_of):
            def one(way, _):
                landed(self.copies(p, way, 0))
                row = self.row(1 + 2 * way, z_of, way)
                encode(
                    lambda b: row, 1, self.half, self.bufs[0].at[p, way, 2], self.bufs[2].at[p, way, 2],
                    adder(self.half, self.bufs[1].at[p, way, 0], self.bufs[3].at[p, way, 0]),
                )
                start(self.copies(p, way, 1))
                return 0

            lax.fori_loop(0, 2, one, 0)

        def finish(self, p, z_of, put):
            for way in range(2):
                landed(self.copies(p, way, 1))

            def one(half, _):
                one = adder(self.half, self.bufs[1].at[p, half, 2], self.bufs[3].at[p, half, 2])
                two = adder(self.half, self.bufs[1].at[p, 1 - half, 1], self.bufs[3].at[p, 1 - half, 1])
                row = self.row(0, z_of, half)
                for r in pieces(self.half):
                    put(row, half, r, part[at_row(row, r), :] + one(0, r) + two(0, r))
                return 0

            lax.fori_loop(0, 2, one, 0)

    class Chain:
        def __init__(self, half, first, x_of, blocks, bufs, recv_sem, kind):
            self.half, self.first, self.x_of, self.blocks = half, first, x_of, blocks
            self.bufs, self.recv_sem, self.kind = bufs, recv_sem, kind

        def copies(self, p, half, slot):
            step = (1 if half == 0 else NZ - 1) if p == 0 else (1 if p % 2 else NZ - 1)
            return message(self.bufs, (slot, half), (p, half), (slot, half), self.kind, self.recv_sem, at_z(step))

        def begin(self):
            for half in range(2):
                self.hop(0, half)

        def hop(self, p, half):
            takes = p >= 3 or (p >= 1 and half == 1 - p % 2)
            if takes:
                landed(self.copies(p, half, p - 1))

            def row_of(b):
                return base(self.x_of(b), zeta(z, p)) + self.first + half * self.half

            encode(
                row_of, self.blocks, self.half, self.bufs[0].at[p, half], self.bufs[2].at[p, half],
                adder(self.half, self.bufs[1].at[p - 1, half], self.bufs[3].at[p - 1, half]) if takes else None,
            )
            start(self.copies(p, half, p + 1 if p else half))

        def finish(self, put):
            for half in range(2):
                for slot in (NZ - 2, NZ - 1):
                    landed(self.copies(0, half, slot))
                one, two = (
                    adder(self.half, self.bufs[1].at[slot, half], self.bufs[3].at[slot, half]) for slot in (NZ - 2, NZ - 1)
                )

                def block(b, _):
                    row = base(self.x_of(b), z) + self.first + half * self.half
                    for r in pieces(self.half):
                        put(row, half, r, part[at_row(row, r), :] + one(b, r) + two(b, r))
                    return 0

                loop(self.blocks, block, 0)

    ring1 = Ring(H1, 0, (xs1, xr1, xss1, xrs1), x1_recv, 0)
    chain1 = Chain(H1, 0, lambda b: x, 1, (zs1, zr1, zss1, zrs1), z1_recv, 1)
    ring2 = Ring(H2, ROWS1, (xs2, xr2, xss2, xrs2), x2_recv, 2)
    chain2 = Chain(H2, ROWS1, lambda b: b, NX, (zs2, zr2, zss2, zrs2), z2_recv, 3)

    def keep(row, half, r, value):
        part[at_row(row, r), :] = value

    def put1(row, half, r, value):
        out_ref[half * H1 + r : half * H1 + r + 16, :] = value

    def put2(row, half, r, value):
        out_ref[at_row(ROWS1 + half * H2, r), :] = value

    for task in ORDER:
        kind, p = task[0], int(task[1:2] or 0)
        if kind == "M":
            multiply(p)
        elif kind == "A":
            ring1.own(p, zeta(z, p))
        elif kind == "B":
            ring1.pass_on(p, zeta(z, p))
        elif kind == "C":
            ring1.finish(p, zeta(z, p), keep)
        elif kind == "Z":
            chain1.hop(p, p % 2)
            chain1.hop(p, 1 - p % 2)
        elif kind == "H" and p == 0:
            chain2.begin()
        elif kind == "H":
            chain2.hop(p, p % 2 if task[2] == "0" else 1 - p % 2)
        elif kind == "E":
            chain2.finish(keep)
        elif kind == "F":
            ring2.own(0, z)
        elif kind == "G":
            ring2.pass_on(0, z)
        elif kind == "I":
            ring2.finish(0, z, put2)
    chain1.finish(put1)

    gp_copy.wait_send()
    pltpu.make_async_remote_copy(
        norms.at[0:7], norms.at[0:7], n_send, n_send, device_id=at_x(1), device_id_type=MESH
    ).wait_send()
    for chain_or_ring in (ring1, chain1, ring2, chain2):
        drain(chain_or_ring.bufs, chain_or_ring.kind)


def per_device(activations, cotangents, doc_ids):
    length, half_kv = activations.shape[1], cotangents.shape[2]
    sections = lax.axis_size("section")
    dma = pltpu.SemaphoreType.DMA
    units1, units2 = (STEPS, 2, 3), (1, 2, 3)
    hops, slots = (STEPS - 1, 2), (STEPS, 2)

    def buffers(ours, theirs, rows):
        return [pltpu.VMEM(s + (rows, half_kv), I16) for s in (ours, theirs)] + [
            pltpu.VMEM(s + (8, 128), F32) for s in (ours, theirs)
        ]

    grad, clip = pl.pallas_call(
        kernel,
        out_shape=(
            jax.ShapeDtypeStruct((BLOCK, half_kv), F32),
            jax.ShapeDtypeStruct((1, DOCS), F32),
        ),
        in_specs=[
            pl.BlockSpec(memory_space=pl.ANY),
            pl.BlockSpec(memory_space=pl.ANY),
            pl.BlockSpec(memory_space=pltpu.VMEM),
        ],
        out_specs=[pl.BlockSpec(memory_space=pltpu.VMEM)] * 2,
        scratch_shapes=[
            pltpu.VMEM((length, D), BF16),
            pltpu.VMEM((D, length), BF16),
            pltpu.VMEM((length, half_kv), BF16),
            pltpu.VMEM((length, half_kv), BF16),
            pltpu.VMEM((D, half_kv), F32),
            pltpu.VMEM((length, half_kv), BF16),
            pltpu.VMEM((2 * sections + length // 128, DOCS, 128), F32),
            pltpu.VMEM((2, 384, 256), F32),
            pltpu.VMEM((2, 384, 256), F32),
            *buffers(units1, units1, H1),
            *buffers(hops, slots, H1),
            *buffers(units2, units2, H2),
            *buffers(hops, slots, NX * H2),
            dma((D // K_CHUNK + 3,)),
            dma(()),
            dma((2,)),
            dma(()),
            dma((7,)),
            dma((4, 2)),
            dma((STEPS, 2, 2, 2)),
            dma(slots + (2,)),
            dma((1, 2, 2, 2)),
            dma(slots + (2,)),
        ],
        compiler_params=pltpu.CompilerParams(
            collective_id=0, has_side_effects=True, vmem_limit_bytes=63 << 20
        ),
        name="clip_and_reduce",
    )(activations[0], cotangents[0], doc_ids)
    return grad[None], clip


def solution(mesh):
    return jax.shard_map(
        per_device,
        mesh=mesh,
        in_specs=(P("section", "dp", None), P("section", "dp", "tensor"), P("dp", None)),
        out_specs=(P("section", "dp", "tensor"), P("dp", None)),
        check_vma=False,
    )
```

```python
import functools
import math

import jax
import jax.numpy as jnp
from jax import lax
from jax.experimental import pallas as pl
from jax.experimental.pallas import tpu as pltpu
from jax.sharding import PartitionSpec as P

D = 5120
KV = 1024
DOCS = 16
CLIP_TOK = 192

F32 = jnp.float32
BF16 = jnp.bfloat16
I16 = jnp.int16
MESH = pl.DeviceIdType.MESH
TOP = 32767.0
TINY = 1e-30

NX, NZ = 4, 8
BLOCK = D // (NX * NZ)
ROWS1, ROWS2 = 96, 64
H1, H2 = ROWS1 // 2, ROWS2 // 2
STEPS = NZ
K_CHUNK = 1280
UNROLL = 4
TRANSPOSE_EARLY = True
ORDER = (
    "M0", "A0", "H00", "M1", "H10", "A1", "M2", "H20", "A2", "M3", "B0", "A3", "M4", "H11", "H21", "A4", "M5", "B1", "M6",
    "H30", "B2", "A5", "H40", "M7", "C0", "Z0", "A7", "A6", "H31", "H41", "B3", "H50", "H60", "B4", "C1", "Z1", "C2", "Z2",
    "H51", "H61", "B5", "B7", "B6", "C3", "Z3", "C4", "Z4", "E", "F", "C5", "C7", "Z5", "C6", "Z6", "G", "I",
)


def nt(a, b):
    return lax.dot_general(a, b, (((1,), (1,)), ((), ())), preferred_element_type=F32)


def tn(a, b, precision=None):
    return lax.dot_general(a, b, (((0,), (0,)), ((), ())), preferred_element_type=F32, precision=precision)


def zeta(z, p):
    odd = p % 2
    return (z + 4 + (1 - odd) * (p // 2) - odd * ((p + 1) // 2)) % NZ


def kernel(
    a_hbm, g_hbm, ids_ref, out_ref,
    a, at, g, gp, part, scaled, norms, acts, cots, ruler,
    xs1, xr1, xss1, xrs1, zs1, zr1, zss1, zrs1,
    xs2, xr2, xss2, xrs2, zs2, zr2, zss2, zrs2,
    a_sem, g_sem, gp_sem, n_send, n_recv, sent, x1_recv, z1_recv, x2_recv, z2_recv,
):
    length = a.shape[0]
    sections = lax.axis_size("section")
    y, dp, core = lax.axis_index("section"), lax.axis_index("dp"), lax.axis_index("tensor")
    x, z = dp // NZ, dp % NZ

    def at_x(step):
        return (y, ((x + step) % NX) * NZ + z, core)

    def at_z(step):
        return (y, x * NZ + (z + step) % NZ, core)

    group = [((y + i) % sections, dp, (core + j) % 2) for i in range(4) for j in range(2) if i or j]
    chunks = D // K_CHUNK
    first = pl.multiple_of(384 * core, 128)
    rest = pl.multiple_of(640 * (1 - core), 128)

    def a_copy(k):
        if k < chunks:
            where = (pl.ds(first, 640), pl.ds(k * K_CHUNK, K_CHUNK))
        else:
            where = (pl.ds(pl.multiple_of(rest + 128 * (k - chunks), 128), 128), pl.ds(0, D))
        return pltpu.make_async_copy(a_hbm.at[where], a.at[where], a_sem.at[k])

    g_copy = pltpu.make_async_copy(g_hbm, g, g_sem)
    g_copy.start()
    for k in range(2):
        a_copy(k).start()

    barrier = pltpu.get_barrier_semaphore()
    for peer in group + [at_x(1), at_x(NX - 1), at_z(1), at_z(NZ - 1)]:
        pl.semaphore_signal(barrier, inc=1, device_id=peer, device_id_type=MESH)

    one_hot = (lax.broadcasted_iota(jnp.int32, (DOCS, length), 0) == ids_ref[...]).astype(F32)
    for k in range(length // 128):
        norms[2 * sections + k] = one_hot[:, k * 128 : (k + 1) * 128]

    def hot(start, count):
        return jnp.concatenate([norms[2 * sections + start + k] for k in range(count)], axis=1)

    def tokens(j):
        u0 = pl.multiple_of(512 * core + 256 * j, 128)
        return pl.multiple_of(jnp.maximum(u0 - 128, 0), 128), u0

    other_row = pl.multiple_of(384 * (1 - core), 128)
    gp_copy = pltpu.make_async_remote_copy(
        g_hbm.at[pl.ds(other_row, 640)], gp.at[pl.ds(other_row, 640)], gp_sem.at[0], gp_sem.at[1],
        device_id=(y, dp, 1 - core), device_id_type=MESH,
    )

    g_copy.wait()
    for j in range(2):
        t0, u0 = tokens(j)
        cots[j] = nt(g[pl.ds(t0, 384), :], g[pl.ds(u0, 256), :])

    for k in range(chunks):
        a_copy(k).wait()
        if k + 2 < chunks:
            a_copy(k + 2).start()
        elif k + 2 == chunks:
            for i in range(3):
                a_copy(chunks + i).start()
        if k == 1:
            pl.semaphore_wait(barrier, len(group) + 4)
            gp_copy.start()
        column = k * K_CHUNK
        for j in range(2):
            t0, u0 = tokens(j)
            product = nt(a[pl.ds(t0, 384), pl.ds(column, K_CHUNK)], a[pl.ds(u0, 256), pl.ds(column, K_CHUNK)])
            acts[j] = product if k == 0 else acts[j] + product
        for lane in range(column, column + K_CHUNK, 128) if TRANSPOSE_EARLY else ():
            at[lane : lane + 128, pl.ds(first, 640)] = a[pl.ds(first, 640), lane : lane + 128].T

    gp_copy.wait_recv()
    total = jnp.zeros((DOCS, 256), F32)
    for j in range(2):
        t0, u0 = tokens(j)
        cot = cots[j] + nt(gp[pl.ds(t0, 384), :], gp[pl.ds(u0, 256), :])
        hot_u = hot(u0 // 128, 2)
        same = tn(hot(t0 // 128, 3), hot_u)
        t = lax.broadcasted_iota(jnp.int32, (384, 256), 0) + t0
        weight = jnp.where(t < u0, 2.0, jnp.where(t < u0 + 256, 1.0, 0.0))
        product = jnp.where(same > 0.5, acts[j] * cot * weight, 0.0)
        total = total + hot_u * jnp.sum(product, axis=0, keepdims=True)
    mine = y * 2 + core
    norms[mine] = total[:, :128] + total[:, 128:]
    n_copies = [
        pltpu.make_async_remote_copy(
            norms.at[mine], norms.at[mine], n_send, n_recv.at[i], device_id=peer, device_id_type=MESH
        )
        for i, peer in enumerate(group)
    ]
    for copy in n_copies:
        copy.start()

    for i in range(3):
        a_copy(chunks + i).wait()

    def transpose(i, _):
        lane = pl.multiple_of(i * 128, 128)
        if not TRANSPOSE_EARLY:
            at[pl.ds(lane, 128), pl.ds(first, 640)] = a[pl.ds(first, 640), pl.ds(lane, 128)].T
        at[pl.ds(lane, 128), pl.ds(rest, 384)] = a[pl.ds(rest, 384), pl.ds(lane, 128)].T
        return 0

    lax.fori_loop(0, D // 128, transpose, 0)

    for copy in n_copies:
        copy.wait_recv()
    norm_sq = norms[0]
    for i in range(1, 2 * sections):
        norm_sq = norm_sq + norms[i]
    norm_sq = jnp.broadcast_to(jnp.sum(norm_sq, axis=1, keepdims=True), (DOCS, 128))
    bound = math.sqrt(4.0 * CLIP_TOK * sections * D * KV)
    clip = jnp.minimum(1.0, bound * lax.rsqrt(norm_sq + 1e-06))
    out_ref[BLOCK : BLOCK + DOCS, :128] = clip
    factor = clip * (1.0 / math.sqrt(NX * NZ * length))
    for k in range(length // 128):
        fac = tn(norms[2 * sections + k], factor, lax.Precision.HIGHEST)
        for lane in range(0, KV // 2, 128):
            own = g[k * 128 : (k + 1) * 128, lane : lane + 128].astype(F32)
            scaled[k * 128 : (k + 1) * 128, lane : lane + 128] = (own * fac).astype(BF16)

    def base(x_of, z_of):
        return (x_of * NZ + z_of) * BLOCK

    def multiply(p):
        def one(i, _):
            row = pl.multiple_of(base(i, zeta(z, p)), 32)
            part[pl.ds(row, BLOCK), :] = jnp.dot(at[pl.ds(row, BLOCK), :], scaled[...], preferred_element_type=F32)
            return 0

        lax.fori_loop(0, NX, one, 0, unroll=UNROLL)

    def at_row(row, r):
        return pl.ds(pl.multiple_of(row + r, 16), 16)

    def pieces(rows):
        return range(0, rows, 16)

    def loop(count, body, carry):
        return body(0, carry) if count == 1 else lax.fori_loop(0, count, body, carry)

    def fold(m, value):
        value = jnp.abs(value)
        for r in range(0, value.shape[0], 8):
            for c in range(0, value.shape[1], 128):
                m = jnp.maximum(m, value[r : r + 8, c : c + 128])
        return m

    def spread(scale):
        return jnp.concatenate([scale] * (KV // 2 // 128), axis=1)

    def encode(row_of, blocks, count, code, scale_ref, add=None):
        def largest(b, m):
            for r in pieces(count):
                value = part[at_row(row_of(b), r), :]
                if add is not None:
                    value = value + add(b, r)
                    part[at_row(row_of(b), r), :] = value
                m = fold(m, value)
            return m

        m = loop(blocks, largest, jnp.zeros((8, 128), F32))
        m = jnp.maximum(jnp.max(m, axis=0, keepdims=True), TINY)
        scale_ref[...] = jnp.broadcast_to(m * (1.0 / TOP), (8, 128))
        inverse = spread(TOP / m)

        def put(b, _):
            for r in pieces(count):
                value = part[at_row(row_of(b), r), :]
                code[at_row(b * count, r), :] = jnp.round(value * inverse).astype(jnp.int32).astype(I16)
            return 0

        loop(blocks, put, 0)

    def adder(count, code, scale_ref):
        scale = spread(scale_ref[0:1, :])
        return lambda b, r: code[at_row(b * count, r), :].astype(jnp.int32).astype(F32) * scale

    def message(bufs, there, here, slot, kind, recv_sem, peer):
        code, got, scale, got_scale = bufs
        one = (slice(0, 1),)
        return [
            pltpu.make_async_remote_copy(
                code.at[here], got.at[there], sent.at[kind, 0], recv_sem.at[slot], device_id=peer, device_id_type=MESH
            ),
            pltpu.make_async_remote_copy(
                scale.at[here + one], got_scale.at[there + one], sent.at[kind, 1], recv_sem.at[slot],
                device_id=peer, device_id_type=MESH,
            ),
        ]

    def start(copies):
        for copy in copies:
            copy.start()

    def landed(rows, recv_sem):
        here = ruler.at[pl.ds(0, rows)]
        pltpu.make_async_remote_copy(
            here, here, recv_sem, recv_sem, device_id=at_x(1), device_id_type=MESH
        ).wait_recv()

    def drain(bufs, kind):
        everything = (slice(None),) * (len(bufs[2].shape) - 2)
        for i, ref in enumerate((bufs[0], bufs[2].at[everything + (slice(0, 1),)])):
            pltpu.make_async_remote_copy(
                ref, ref, sent.at[kind, i], sent.at[kind, i], device_id=at_x(1), device_id_type=MESH
            ).wait_send()

    class Ring:
        def __init__(self, half, first, bufs, recv_sem, kind):
            self.half, self.first, self.bufs, self.recv_sem, self.kind = half, first, bufs, recv_sem, kind

        def copies(self, p, way, late):
            units = (p, way, pl.ds(2, 1) if late else pl.ds(0, 2))
            return message(self.bufs, units, units, (p, way, late), self.kind, self.recv_sem, at_x(1 + 2 * way))

        def landed(self, p, way, late):
            landed((2 - late) * (2 * self.half + 1), self.recv_sem.at[p, way, late])

        def row(self, step, z_of, half):
            return base((x + step) % NX, z_of) + self.first + half * self.half

        def own(self, p, z_of):
            def one(way, _):
                for unit in range(2):
                    row = self.row(1 + 2 * way, z_of, 1 - way) if unit else self.row(2, z_of, way)
                    encode(lambda b: row, 1, self.half, self.bufs[0].at[p, way, unit], self.bufs[2].at[p, way, unit])
                start(self.copies(p, way, 0))
                return 0

            lax.fori_loop(0, 2, one, 0)

        def pass_on(self, p, z_of):
            def one(way, _):
                self.landed(p, way, 0)
                row = self.row(1 + 2 * way, z_of, way)
                encode(
                    lambda b: row, 1, self.half, self.bufs[0].at[p, way, 2], self.bufs[2].at[p, way, 2],
                    adder(self.half, self.bufs[1].at[p, way, 0], self.bufs[3].at[p, way, 0]),
                )
                start(self.copies(p, way, 1))
                return 0

            lax.fori_loop(0, 2, one, 0)

        def finish(self, p, z_of, put):
            for way in range(2):
                self.landed(p, way, 1)

            def one(half, _):
                one = adder(self.half, self.bufs[1].at[p, half, 2], self.bufs[3].at[p, half, 2])
                two = adder(self.half, self.bufs[1].at[p, 1 - half, 1], self.bufs[3].at[p, 1 - half, 1])
                row = self.row(0, z_of, half)
                for r in pieces(self.half):
                    put(row, half, r, part[at_row(row, r), :] + one(0, r) + two(0, r))
                return 0

            lax.fori_loop(0, 2, one, 0)

    class Chain:
        def __init__(self, half, first, x_of, blocks, bufs, recv_sem, kind):
            self.half, self.first, self.x_of, self.blocks = half, first, x_of, blocks
            self.bufs, self.recv_sem, self.kind = bufs, recv_sem, kind

        def copies(self, p, half, slot):
            step = (1 if half == 0 else NZ - 1) if p == 0 else (1 if p % 2 else NZ - 1)
            return message(self.bufs, (slot, half), (p, half), (slot, half), self.kind, self.recv_sem, at_z(step))

        def landed(self, slot, half):
            landed(2 * self.blocks * self.half + 1, self.recv_sem.at[slot, half])

        def begin(self):
            for half in range(2):
                self.hop(0, half)

        def hop(self, p, half):
            takes = p >= 3 or (p >= 1 and half == 1 - p % 2)
            if takes:
                self.landed(p - 1, half)

            def row_of(b):
                return base(self.x_of(b), zeta(z, p)) + self.first + half * self.half

            encode(
                row_of, self.blocks, self.half, self.bufs[0].at[p, half], self.bufs[2].at[p, half],
                adder(self.half, self.bufs[1].at[p - 1, half], self.bufs[3].at[p - 1, half]) if takes else None,
            )
            start(self.copies(p, half, p + 1 if p else half))

        def finish(self, put):
            for half in range(2):
                for slot in (NZ - 2, NZ - 1):
                    self.landed(slot, half)
                one, two = (
                    adder(self.half, self.bufs[1].at[slot, half], self.bufs[3].at[slot, half]) for slot in (NZ - 2, NZ - 1)
                )

                def block(b, _):
                    row = base(self.x_of(b), z) + self.first + half * self.half
                    for r in pieces(self.half):
                        put(row, half, r, part[at_row(row, r), :] + one(b, r) + two(b, r))
                    return 0

                loop(self.blocks, block, 0)

    ring1 = Ring(H1, 0, (xs1, xr1, xss1, xrs1), x1_recv, 0)
    chain1 = Chain(H1, 0, lambda b: x, 1, (zs1, zr1, zss1, zrs1), z1_recv, 1)
    ring2 = Ring(H2, ROWS1, (xs2, xr2, xss2, xrs2), x2_recv, 2)
    chain2 = Chain(H2, ROWS1, lambda b: b, NX, (zs2, zr2, zss2, zrs2), z2_recv, 3)

    def keep(row, half, r, value):
        part[at_row(row, r), :] = value

    def put1(row, half, r, value):
        out_ref[half * H1 + r : half * H1 + r + 16, :] = value

    def put2(row, half, r, value):
        out_ref[at_row(ROWS1 + half * H2, r), :] = value

    for task in ORDER:
        kind, p = task[0], int(task[1:2] or 0)
        if kind == "M":
            multiply(p)
        elif kind == "A":
            ring1.own(p, zeta(z, p))
        elif kind == "B":
            ring1.pass_on(p, zeta(z, p))
        elif kind == "C":
            ring1.finish(p, zeta(z, p), keep)
        elif kind == "Z":
            chain1.hop(p, p % 2)
            chain1.hop(p, 1 - p % 2)
        elif kind == "H" and p == 0:
            chain2.begin()
        elif kind == "H":
            chain2.hop(p, p % 2 if task[2] == "0" else 1 - p % 2)
        elif kind == "E":
            chain2.finish(keep)
        elif kind == "F":
            ring2.own(0, z)
        elif kind == "G":
            ring2.pass_on(0, z)
        elif kind == "I":
            ring2.finish(0, z, put2)
    chain1.finish(put1)

    gp_copy.wait_send()
    pltpu.make_async_remote_copy(
        norms.at[0:7], norms.at[0:7], n_send, n_send, device_id=at_x(1), device_id_type=MESH
    ).wait_send()
    for chain_or_ring in (ring1, chain1, ring2, chain2):
        drain(chain_or_ring.bufs, chain_or_ring.kind)


def take_apart(result_ref, grad_ref, clip_ref):
    grad_ref[0] = result_ref[:BLOCK, :]
    clip_ref[...] = result_ref[BLOCK:, :128].T[:1, :]


def per_device(activations, cotangents, doc_ids):
    length, half_kv = activations.shape[1], cotangents.shape[2]
    sections = lax.axis_size("section")
    dma = pltpu.SemaphoreType.DMA
    units1, units2 = (STEPS, 2, 3), (1, 2, 3)
    hops, slots = (STEPS - 1, 2), (STEPS, 2)

    def buffers(ours, theirs, rows):
        return [pltpu.VMEM(s + (rows, half_kv), I16) for s in (ours, theirs)] + [
            pltpu.VMEM(s + (8, 128), F32) for s in (ours, theirs)
        ]

    result = pl.pallas_call(
        kernel,
        out_shape=jax.ShapeDtypeStruct((BLOCK + DOCS, half_kv), F32),
        in_specs=[
            pl.BlockSpec(memory_space=pl.ANY),
            pl.BlockSpec(memory_space=pl.ANY),
            pl.BlockSpec(memory_space=pltpu.VMEM),
        ],
        out_specs=pl.BlockSpec(memory_space=pltpu.VMEM),
        scratch_shapes=[
            pltpu.VMEM((length, D), BF16),
            pltpu.VMEM((D, length), BF16),
            pltpu.VMEM((length, half_kv), BF16),
            pltpu.VMEM((length, half_kv), BF16),
            pltpu.VMEM((D, half_kv), F32),
            pltpu.VMEM((length, half_kv), BF16),
            pltpu.VMEM((2 * sections + length // 128, DOCS, 128), F32),
            pltpu.VMEM((2, 384, 256), F32),
            pltpu.VMEM((2, 384, 256), F32),
            pltpu.VMEM((2 * NX * H2 + 8, 128), F32),
            *buffers(units1, units1, H1),
            *buffers(hops, slots, H1),
            *buffers(units2, units2, H2),
            *buffers(hops, slots, NX * H2),
            dma((D // K_CHUNK + 3,)),
            dma(()),
            dma((2,)),
            dma(()),
            dma((7,)),
            dma((4, 2)),
            dma((STEPS, 2, 2)),
            dma(slots),
            dma((1, 2, 2)),
            dma(slots),
        ],
        compiler_params=pltpu.CompilerParams(
            collective_id=0, has_side_effects=True, vmem_limit_bytes=63 << 20
        ),
        name="clip_and_reduce",
    )(activations[0], cotangents[0], doc_ids)
    return pl.pallas_call(
        take_apart,
        out_shape=(
            jax.ShapeDtypeStruct((1, BLOCK, half_kv), F32),
            jax.ShapeDtypeStruct((1, DOCS), F32),
        ),
        in_specs=[pl.BlockSpec(memory_space=pltpu.VMEM)],
        out_specs=[pl.BlockSpec(memory_space=pltpu.VMEM)] * 2,
        name="take_apart",
    )(result)


def solution(mesh):
    return jax.shard_map(
        per_device,
        mesh=mesh,
        in_specs=(P("section", "dp", None), P("section", "dp", "tensor"), P("dp", None)),
        out_specs=(P("section", "dp", "tensor"), P("dp", None)),
        check_vma=False,
    )
```

```python
import functools
import math

import jax
import jax.numpy as jnp
from jax import lax
from jax.experimental import pallas as pl
from jax.experimental.pallas import tpu as pltpu
from jax.sharding import PartitionSpec as P

D = 5120
KV = 1024
DOCS = 16
CLIP_TOK = 192

F32 = jnp.float32
BF16 = jnp.bfloat16
I16 = jnp.int16
MESH = pl.DeviceIdType.MESH
TOP = 32767.0
TINY = 1e-30

NX, NZ = 4, 8
BLOCK = D // (NX * NZ)
ROWS1, ROWS2 = 96, 64
H1, H2 = ROWS1 // 2, ROWS2 // 2
STEPS = NZ
K_CHUNK = 1280
AHEAD = 3
TRANSPOSE_EARLY = True
ORDER = (
    "P", "H00", "M1", "A1", "H10", "M2", "H20", "A2", "M3", "M4", "B0", "A4", "A3", "M5", "H21", "H11", "M6", "M7", "H30",
    "H40", "B1", "B2", "A6", "A5", "A7", "C0", "Z0", "H41", "H31", "B4", "B3", "H60", "H50", "C1", "Z1", "C2", "Z2", "H61",
    "H51", "B6", "B5", "B7", "C4", "Z4", "C3", "Z3", "C6", "E", "F", "C5", "C7", "Z6", "Z5", "G", "I",
)


def nt(a, b):
    return lax.dot_general(a, b, (((1,), (1,)), ((), ())), preferred_element_type=F32)


def tn(a, b, precision=None):
    return lax.dot_general(a, b, (((0,), (0,)), ((), ())), preferred_element_type=F32, precision=precision)


def zeta(z, p):
    odd = p % 2
    return (z + 4 + (1 - odd) * (p // 2) - odd * ((p + 1) // 2)) % NZ


def kernel(
    a_hbm, g_hbm, ids_ref, out_ref,
    a, at, g, gp, part, scaled, norms, acts, cots, ruler,
    xs1, xr1, xss1, xrs1, zs1, zr1, zss1, zrs1,
    xs2, xr2, xss2, xrs2, zs2, zr2, zss2, zrs2,
    a_sem, g_sem, gp_sem, n_send, n_recv, sent, x1_recv, z1_recv, x2_recv, z2_recv,
):
    length = a.shape[0]
    sections = lax.axis_size("section")
    y, dp, core = lax.axis_index("section"), lax.axis_index("dp"), lax.axis_index("tensor")
    x, z = dp // NZ, dp % NZ

    def at_x(step):
        return (y, ((x + step) % NX) * NZ + z, core)

    def at_z(step):
        return (y, x * NZ + (z + step) % NZ, core)

    group = [((y + i) % sections, dp, (core + j) % 2) for i in range(4) for j in range(2) if i or j]
    chunks = D // K_CHUNK
    first = pl.multiple_of(384 * core, 128)
    rest = pl.multiple_of(640 * (1 - core), 128)

    def a_copy(k):
        if k < chunks:
            where = (pl.ds(first, 640), pl.ds(k * K_CHUNK, K_CHUNK))
        else:
            where = (pl.ds(pl.multiple_of(rest + 128 * (k - chunks), 128), 128), pl.ds(0, D))
        return pltpu.make_async_copy(a_hbm.at[where], a.at[where], a_sem.at[k])

    g_copy = pltpu.make_async_copy(g_hbm, g, g_sem)
    g_copy.start()
    for k in range(AHEAD):
        a_copy(k).start()

    barrier = pltpu.get_barrier_semaphore()
    for peer in group + [at_x(1), at_x(NX - 1), at_z(1), at_z(NZ - 1)]:
        pl.semaphore_signal(barrier, inc=1, device_id=peer, device_id_type=MESH)

    one_hot = (lax.broadcasted_iota(jnp.int32, (DOCS, length), 0) == ids_ref[...]).astype(F32)
    for k in range(length // 128):
        norms[2 * sections + k] = one_hot[:, k * 128 : (k + 1) * 128]

    def hot(start, count):
        return jnp.concatenate([norms[2 * sections + start + k] for k in range(count)], axis=1)

    def tokens(j):
        u0 = pl.multiple_of(512 * core + 256 * j, 128)
        return pl.multiple_of(jnp.maximum(u0 - 128, 0), 128), u0

    other_row = pl.multiple_of(384 * (1 - core), 128)
    gp_copy = pltpu.make_async_remote_copy(
        g_hbm.at[pl.ds(other_row, 640)], gp.at[pl.ds(other_row, 640)], gp_sem.at[0], gp_sem.at[1],
        device_id=(y, dp, 1 - core), device_id_type=MESH,
    )

    g_copy.wait()
    for j in range(2):
        t0, u0 = tokens(j)
        cots[j] = nt(g[pl.ds(t0, 384), :], g[pl.ds(u0, 256), :])

    for k in range(chunks):
        a_copy(k).wait()
        if k + AHEAD < chunks:
            a_copy(k + AHEAD).start()
        elif k + AHEAD == chunks:
            for i in range(3):
                a_copy(chunks + i).start()
        if k == 1:
            pl.semaphore_wait(barrier, len(group) + 4)
            gp_copy.start()
        column = k * K_CHUNK
        for j in range(2):
            t0, u0 = tokens(j)
            product = nt(a[pl.ds(t0, 384), pl.ds(column, K_CHUNK)], a[pl.ds(u0, 256), pl.ds(column, K_CHUNK)])
            acts[j] = product if k == 0 else acts[j] + product
        for lane in range(column, column + K_CHUNK, 128) if TRANSPOSE_EARLY else ():
            at[lane : lane + 128, pl.ds(first, 640)] = a[pl.ds(first, 640), lane : lane + 128].T

    gp_copy.wait_recv()
    total = jnp.zeros((DOCS, 256), F32)
    for j in range(2):
        t0, u0 = tokens(j)
        cot = cots[j] + nt(gp[pl.ds(t0, 384), :], gp[pl.ds(u0, 256), :])
        hot_u = hot(u0 // 128, 2)
        same = tn(hot(t0 // 128, 3), hot_u)
        t = lax.broadcasted_iota(jnp.int32, (384, 256), 0) + t0
        weight = jnp.where(t < u0, 2.0, jnp.where(t < u0 + 256, 1.0, 0.0))
        product = jnp.where(same > 0.5, acts[j] * cot * weight, 0.0)
        total = total + hot_u * jnp.sum(product, axis=0, keepdims=True)
    mine = y * 2 + core
    norms[mine] = total[:, :128] + total[:, 128:]
    n_copies = [
        pltpu.make_async_remote_copy(
            norms.at[mine], norms.at[mine], n_send, n_recv.at[i], device_id=peer, device_id_type=MESH
        )
        for i, peer in enumerate(group)
    ]
    for copy in n_copies:
        copy.start()

    for i in range(3):
        a_copy(chunks + i).wait()

    def transpose(i, _):
        lane = pl.multiple_of(i * 128, 128)
        if not TRANSPOSE_EARLY:
            at[pl.ds(lane, 128), pl.ds(first, 640)] = a[pl.ds(first, 640), pl.ds(lane, 128)].T
        at[pl.ds(lane, 128), pl.ds(rest, 384)] = a[pl.ds(rest, 384), pl.ds(lane, 128)].T
        return 0

    lax.fori_loop(0, D // 128, transpose, 0, unroll=4)

    for copy in n_copies:
        copy.wait_recv()
    norm_sq = norms[0]
    for i in range(1, 2 * sections):
        norm_sq = norm_sq + norms[i]
    norm_sq = jnp.broadcast_to(jnp.sum(norm_sq, axis=1, keepdims=True), (DOCS, 128))
    bound = math.sqrt(4.0 * CLIP_TOK * sections * D * KV)
    clip = jnp.minimum(1.0, bound * lax.rsqrt(norm_sq + 1e-06))
    out_ref[BLOCK : BLOCK + DOCS, :128] = clip
    factor = clip * (1.0 / math.sqrt(NX * NZ * length))
    for k in range(length // 128):
        fac = tn(norms[2 * sections + k], factor, lax.Precision.HIGHEST)
        for lane in range(0, KV // 2, 128):
            own = g[k * 128 : (k + 1) * 128, lane : lane + 128].astype(F32)
            scaled[k * 128 : (k + 1) * 128, lane : lane + 128] = (own * fac).astype(BF16)

    def base(x_of, z_of):
        return (x_of * NZ + z_of) * BLOCK

    def multiply(p, steps=(0, 1, 2, 3)):
        for step in steps:
            row = pl.multiple_of(base((x + step) % NX, zeta(z, p)), 32)
            part[pl.ds(row, BLOCK), :] = jnp.dot(at[pl.ds(row, BLOCK), :], scaled[...], preferred_element_type=F32)

    def at_row(row, r):
        return pl.ds(pl.multiple_of(row + r, 16), 16)

    def pieces(rows):
        return range(0, rows, 16)

    def loop(count, body, carry):
        return body(0, carry) if count == 1 else lax.fori_loop(0, count, body, carry)

    def fold(m, value):
        value = jnp.abs(value)
        for r in range(0, value.shape[0], 8):
            for c in range(0, value.shape[1], 128):
                m = jnp.maximum(m, value[r : r + 8, c : c + 128])
        return m

    def spread(scale):
        return jnp.concatenate([scale] * (KV // 2 // 128), axis=1)

    def encode(row_of, blocks, count, code, scale_ref, add=None):
        def largest(b, m):
            for r in pieces(count):
                value = part[at_row(row_of(b), r), :]
                if add is not None:
                    value = value + add(b, r)
                    part[at_row(row_of(b), r), :] = value
                m = fold(m, value)
            return m

        m = loop(blocks, largest, jnp.zeros((8, 128), F32))
        m = jnp.maximum(jnp.max(m, axis=0, keepdims=True), TINY)
        scale_ref[...] = jnp.broadcast_to(m * (1.0 / TOP), (8, 128))
        inverse = spread(TOP / m)

        def put(b, _):
            for r in pieces(count):
                value = part[at_row(row_of(b), r), :]
                code[at_row(b * count, r), :] = jnp.round(value * inverse).astype(jnp.int32).astype(I16)
            return 0

        loop(blocks, put, 0)

    def adder(count, code, scale_ref):
        scale = spread(scale_ref[0:1, :])
        return lambda b, r: code[at_row(b * count, r), :].astype(jnp.int32).astype(F32) * scale

    def message(bufs, there, here, slot, kind, recv_sem, peer):
        code, got, scale, got_scale = bufs
        one = (slice(0, 1),)
        return [
            pltpu.make_async_remote_copy(
                code.at[here], got.at[there], sent.at[kind, 0], recv_sem.at[slot], device_id=peer, device_id_type=MESH
            ),
            pltpu.make_async_remote_copy(
                scale.at[here + one], got_scale.at[there + one], sent.at[kind, 1], recv_sem.at[slot],
                device_id=peer, device_id_type=MESH,
            ),
        ]

    def start(copies):
        for copy in copies:
            copy.start()

    def landed(rows, recv_sem):
        here = ruler.at[pl.ds(0, rows)]
        pltpu.make_async_remote_copy(
            here, here, recv_sem, recv_sem, device_id=at_x(1), device_id_type=MESH
        ).wait_recv()

    def drain(bufs, kind):
        everything = (slice(None),) * (len(bufs[2].shape) - 2)
        for i, ref in enumerate((bufs[0], bufs[2].at[everything + (slice(0, 1),)])):
            pltpu.make_async_remote_copy(
                ref, ref, sent.at[kind, i], sent.at[kind, i], device_id=at_x(1), device_id_type=MESH
            ).wait_send()

    class Ring:
        def __init__(self, half, first, bufs, recv_sem, kind):
            self.half, self.first, self.bufs, self.recv_sem, self.kind = half, first, bufs, recv_sem, kind

        def copies(self, p, way, late):
            units = (p, way, pl.ds(2, 1) if late else pl.ds(0, 2))
            return message(self.bufs, units, units, (p, way, late), self.kind, self.recv_sem, at_x(1 + 2 * way))

        def landed(self, p, way, late):
            landed((2 - late) * (2 * self.half + 1), self.recv_sem.at[p, way, late])

        def row(self, step, z_of, half):
            return base((x + step) % NX, z_of) + self.first + half * self.half

        def own(self, p, z_of):
            lax.fori_loop(0, 2, lambda way, _: self.own_way(p, z_of, way), 0)

        def own_way(self, p, z_of, way):
            for unit in range(2):
                row = self.row(1 + 2 * way, z_of, 1 - way) if unit else self.row(2, z_of, way)
                encode(lambda b: row, 1, self.half, self.bufs[0].at[p, way, unit], self.bufs[2].at[p, way, unit])
            start(self.copies(p, way, 0))
            return 0

        def pass_on(self, p, z_of):
            def one(way, _):
                self.landed(p, way, 0)
                row = self.row(1 + 2 * way, z_of, way)
                encode(
                    lambda b: row, 1, self.half, self.bufs[0].at[p, way, 2], self.bufs[2].at[p, way, 2],
                    adder(self.half, self.bufs[1].at[p, way, 0], self.bufs[3].at[p, way, 0]),
                )
                start(self.copies(p, way, 1))
                return 0

            lax.fori_loop(0, 2, one, 0)

        def finish(self, p, z_of, put):
            for way in range(2):
                self.landed(p, way, 1)

            def one(half, _):
                one = adder(self.half, self.bufs[1].at[p, half, 2], self.bufs[3].at[p, half, 2])
                two = adder(self.half, self.bufs[1].at[p, 1 - half, 1], self.bufs[3].at[p, 1 - half, 1])
                row = self.row(0, z_of, half)
                for r in pieces(self.half):
                    put(row, half, r, part[at_row(row, r), :] + one(0, r) + two(0, r))
                return 0

            lax.fori_loop(0, 2, one, 0)

    class Chain:
        def __init__(self, half, first, x_of, blocks, bufs, recv_sem, kind):
            self.half, self.first, self.x_of, self.blocks = half, first, x_of, blocks
            self.bufs, self.recv_sem, self.kind = bufs, recv_sem, kind

        def copies(self, p, half, slot):
            step = (1 if half == 0 else NZ - 1) if p == 0 else (1 if p % 2 else NZ - 1)
            return message(self.bufs, (slot, half), (p, half), (slot, half), self.kind, self.recv_sem, at_z(step))

        def landed(self, slot, half):
            landed(2 * self.blocks * self.half + 1, self.recv_sem.at[slot, half])

        def begin(self):
            for half in range(2):
                self.hop(0, half)

        def hop(self, p, half):
            takes = p >= 3 or (p >= 1 and half == 1 - p % 2)
            if takes:
                self.landed(p - 1, half)

            def row_of(b):
                return base(self.x_of(b), zeta(z, p)) + self.first + half * self.half

            encode(
                row_of, self.blocks, self.half, self.bufs[0].at[p, half], self.bufs[2].at[p, half],
                adder(self.half, self.bufs[1].at[p - 1, half], self.bufs[3].at[p - 1, half]) if takes else None,
            )
            start(self.copies(p, half, p + 1 if p else half))

        def finish(self, put):
            for half in range(2):
                for slot in (NZ - 2, NZ - 1):
                    self.landed(slot, half)
                one, two = (
                    adder(self.half, self.bufs[1].at[slot, half], self.bufs[3].at[slot, half]) for slot in (NZ - 2, NZ - 1)
                )

                def block(b, _):
                    row = base(self.x_of(b), z) + self.first + half * self.half
                    for r in pieces(self.half):
                        put(row, half, r, part[at_row(row, r), :] + one(b, r) + two(b, r))
                    return 0

                loop(self.blocks, block, 0)

    ring1 = Ring(H1, 0, (xs1, xr1, xss1, xrs1), x1_recv, 0)
    chain1 = Chain(H1, 0, lambda b: x, 1, (zs1, zr1, zss1, zrs1), z1_recv, 1)
    ring2 = Ring(H2, ROWS1, (xs2, xr2, xss2, xrs2), x2_recv, 2)
    chain2 = Chain(H2, ROWS1, lambda b: b, NX, (zs2, zr2, zss2, zrs2), z2_recv, 3)

    def keep(row, half, r, value):
        part[at_row(row, r), :] = value

    def put1(row, half, r, value):
        out_ref[half * H1 + r : half * H1 + r + 16, :] = value

    def put2(row, half, r, value):
        out_ref[at_row(ROWS1 + half * H2, r), :] = value

    for task in ORDER:
        kind, p = task[0], int(task[1:2] or 0)
        if kind == "P":
            multiply(0, (2, 1))
            ring1.own_way(0, zeta(z, 0), 0)
            multiply(0, (3,))
            ring1.own_way(0, zeta(z, 0), 1)
            multiply(0, (0,))
        elif kind == "M":
            multiply(p)
        elif kind == "A":
            ring1.own(p, zeta(z, p))
        elif kind == "B":
            ring1.pass_on(p, zeta(z, p))
        elif kind == "C":
            ring1.finish(p, zeta(z, p), keep)
        elif kind == "Z":
            chain1.hop(p, p % 2)
            chain1.hop(p, 1 - p % 2)
        elif kind == "H" and p == 0:
            chain2.begin()
        elif kind == "H":
            chain2.hop(p, p % 2 if task[2] == "0" else 1 - p % 2)
        elif kind == "E":
            chain2.finish(keep)
        elif kind == "F":
            ring2.own(0, z)
        elif kind == "G":
            ring2.pass_on(0, z)
        elif kind == "I":
            ring2.finish(0, z, put2)
    chain1.finish(put1)

    gp_copy.wait_send()
    pltpu.make_async_remote_copy(
        norms.at[0:7], norms.at[0:7], n_send, n_send, device_id=at_x(1), device_id_type=MESH
    ).wait_send()
    for chain_or_ring in (ring1, chain1, ring2, chain2):
        drain(chain_or_ring.bufs, chain_or_ring.kind)


def take_apart(result_ref, grad_ref, clip_ref, clip, grad_sem, clip_sem):
    grad_copy = pltpu.make_async_copy(result_ref.at[pl.ds(0, BLOCK)], grad_ref.at[0], grad_sem)
    grad_copy.start()
    clip_copy = pltpu.make_async_copy(result_ref.at[pl.ds(BLOCK, DOCS), pl.ds(0, 128)], clip, clip_sem)
    clip_copy.start()
    clip_copy.wait()
    clip_ref[...] = clip[...].T[:1, :]
    grad_copy.wait()


def per_device(activations, cotangents, doc_ids):
    length, half_kv = activations.shape[1], cotangents.shape[2]
    sections = lax.axis_size("section")
    dma = pltpu.SemaphoreType.DMA
    units1, units2 = (STEPS, 2, 3), (1, 2, 3)
    hops, slots = (STEPS - 1, 2), (STEPS, 2)

    def buffers(ours, theirs, rows):
        return [pltpu.VMEM(s + (rows, half_kv), I16) for s in (ours, theirs)] + [
            pltpu.VMEM(s + (8, 128), F32) for s in (ours, theirs)
        ]

    result = pl.pallas_call(
        kernel,
        out_shape=pltpu.VMEM((BLOCK + DOCS, half_kv), F32),
        in_specs=[
            pl.BlockSpec(memory_space=pl.ANY),
            pl.BlockSpec(memory_space=pl.ANY),
            pl.BlockSpec(memory_space=pltpu.VMEM),
        ],
        out_specs=pl.BlockSpec(memory_space=pltpu.VMEM),
        scratch_shapes=[
            pltpu.VMEM((length, D), BF16),
            pltpu.VMEM((D, length), BF16),
            pltpu.VMEM((length, half_kv), BF16),
            pltpu.VMEM((length, half_kv), BF16),
            pltpu.VMEM((D, half_kv), F32),
            pltpu.VMEM((length, half_kv), BF16),
            pltpu.VMEM((2 * sections + length // 128, DOCS, 128), F32),
            pltpu.VMEM((2, 384, 256), F32),
            pltpu.VMEM((2, 384, 256), F32),
            pltpu.VMEM((2 * NX * H2 + 8, 128), F32),
            *buffers(units1, units1, H1),
            *buffers(hops, slots, H1),
            *buffers(units2, units2, H2),
            *buffers(hops, slots, NX * H2),
            dma((D // K_CHUNK + 3,)),
            dma(()),
            dma((2,)),
            dma(()),
            dma((7,)),
            dma((4, 2)),
            dma((STEPS, 2, 2)),
            dma(slots),
            dma((1, 2, 2)),
            dma(slots),
        ],
        compiler_params=pltpu.CompilerParams(
            collective_id=0, has_side_effects=True, vmem_limit_bytes=63 << 20
        ),
        name="clip_and_reduce",
    )(activations[0], cotangents[0], doc_ids)
    return pl.pallas_call(
        take_apart,
        out_shape=(
            jax.ShapeDtypeStruct((1, BLOCK, half_kv), F32),
            jax.ShapeDtypeStruct((1, DOCS), F32),
        ),
        in_specs=[pl.BlockSpec(memory_space=pl.ANY)],
        out_specs=[pl.BlockSpec(memory_space=pl.ANY), pl.BlockSpec(memory_space=pltpu.VMEM)],
        scratch_shapes=[
            pltpu.VMEM((DOCS, 128), F32),
            pltpu.SemaphoreType.DMA(()),
            pltpu.SemaphoreType.DMA(()),
        ],
        compiler_params=pltpu.CompilerParams(vmem_limit_bytes=1 << 20),
        name="take_apart",
    )(result)


def solution(mesh):
    return jax.shard_map(
        per_device,
        mesh=mesh,
        in_specs=(P("section", "dp", None), P("section", "dp", "tensor"), P("dp", None)),
        out_specs=(P("section", "dp", "tensor"), P("dp", None)),
        check_vma=False,
    )
```
